256 devices in a mesh: dp: 8 (over x_hi, y), tensor: 32 (over z, x_lo, core).
Axes of the slice: x: 4 (x_hi: 2, x_lo: 2; x = x_hi * 2 + x_lo), y: 4, z: 8, core: 2. Of those that a mesh axis runs over, the one named last changes fastest.
Arguments:
- hidden: bfloat16 [4096, 16384], P('dp', 'tensor'), may hold values from -6 to 6
- down_weight: bfloat16 [16384, 8192], P('tensor'), may hold values from -0.046875 to 0.046875
- adapter_first_factor: bfloat16 [16384, 1024], P('tensor'), may hold values from -0.046875 to 0.046875
- adapter_second_factor: bfloat16 [1024, 8192], P(None, 'tensor'), may hold values from -1.5 to 1.5
- output_gradient: bfloat16 [4096, 8192], P(('dp', 'tensor')), may hold values from -6 to 6
- token_language_index: int32 [8, 512], P('dp'), may hold values from 0 to 63, never falling along the last dimension, each value on 1 to 128 neighbouring positions
- owned: int32 [64], replicated, may hold values from 0 to 63, each once
Outputs:
- mixed: bfloat16 [4096, 8192], P(('dp', 'tensor'))
- hidden_gradient: bfloat16 [4096, 16384], P('dp', 'tensor')
- grad_a: float32 [64, 16, 16384], P('dp', None, 'tensor')
- grad_b: float32 [64, 16, 8192], P('dp', None, 'tensor')
The draws below stay inside these ranges and needn't reach their ends.
Inputs may be any that keep to these rules, and one draw needn't show every extreme that they name: Each row of token_language_index never falls and names every language; one language has exactly 128 tokens of the row, none more. `owned`: each adapter appears once.
All inputs are finite; a program needn't handle non-finite values.
Results may differ from the reference program's by a relative error of at most 0.0075.
Values may be sent and summed in bfloat16 or wider, within the bound.
A program may use at most 128 MiB of HBM per device.

```python
import math
import jax
import jax.numpy as jnp
import numpy as np

MODEL_WIDTH = 8192
HIDDEN_UNITS = 16384
ADAPTER_RANK = 16
LANGUAGE_COUNT = 64
TOK_GROUP = 512
TOKENS = 4096
RUN_MOST = 128
N_DP = 8


def steps_of(rng, shape, cuts, least, largest):
    def one(axis_at, parts):
        draws = jax.random.uniform(jax.random.fold_in(jax.random.fold_in(rng, 6), axis_at), (parts,), jnp.float32, least / len(cuts), largest / len(cuts))
        return jnp.repeat(jnp.exp(draws), shape[axis_at] // parts).reshape((-1,) + (1,) * (len(shape) - axis_at - 1))

    gain = one(*cuts[0])
    for cut in cuts[1:]:
        gain = gain * one(*cut)
    return gain


def profile(count, total, bound, slope):
    loads = [(1 << 20) // math.isqrt(rank ** slope) + 1 for rank in range(2, count + 1)]
    rest, holding = total - bound - (count - 1), [1] * (count - 1)
    while rest > 0:
        movable = [i for i in range(count - 1) if holding[i] < bound]
        mass, left = sum([loads[i] for i in movable]), rest
        for i in movable:
            addition = min(bound - holding[i], max(1, left * loads[i] // mass), rest)
            holding[i] = holding[i] + addition
            rest = rest - addition
    return np.array([bound] + holding)


def uneven_parts(own_key, amount, total, limit, skew):
    if amount == 2:
        one = jax.random.randint(own_key, (), max(1, total - limit), min(limit, total - 1) + 1)
        return jnp.stack([one, total - one])
    tallies = jnp.asarray(profile(amount, total, limit, skew), jnp.int32)
    pairs = (amount - 1) // 2
    source_of, sink = tallies[1:1 + 2 * pairs:2], tallies[2:2 + 2 * pairs:2]
    margin = jnp.minimum(source_of - 1, limit - sink)
    moved = jax.random.randint(jax.random.fold_in(own_key, 1), (pairs,), 0, 1 << 20) % (margin + 1)
    tallies = tallies.at[1:1 + 2 * pairs:2].set(source_of - moved).at[2:2 + 2 * pairs:2].set(sink + moved)
    return tallies[jax.random.permutation(jax.random.fold_in(own_key, 2), amount)]


def scatter_about(rng, dims, spread, most, shards=(), held_as=jnp.bfloat16):
    result = jax.random.normal(rng, dims, jnp.float32) * spread
    if len(shards) > 0:
        result = steps_of(rng, dims, shards, -0.22, 0.18) * result
    return jnp.clip(result, min=-most, max=most).astype(held_as)


def setup_inputs(seed: int = 0) -> dict:
    seeds = jax.random.split(jax.random.key(seed), 8)
    hidden = scatter_about(seeds[0], (TOKENS, HIDDEN_UNITS), 1.0, 6.0, ((0, 8), (1, 32)))
    down_weight = scatter_about(seeds[1], (HIDDEN_UNITS, MODEL_WIDTH), HIDDEN_UNITS ** -0.5, 0.046875, ((0, 32),))
    adapter_first_factor = scatter_about(seeds[2], (HIDDEN_UNITS, LANGUAGE_COUNT * ADAPTER_RANK), HIDDEN_UNITS ** -0.5, 0.046875, ((0, 32),))
    adapter_second_factor = scatter_about(seeds[3], (LANGUAGE_COUNT * ADAPTER_RANK, MODEL_WIDTH), ADAPTER_RANK ** -0.5, 1.5, ((1, 32),))
    output_gradient = scatter_about(seeds[4], (TOKENS, MODEL_WIDTH), 1.0, 6.0, ((0, 256),))
    token_language_index = jax.vmap(lambda own: jnp.searchsorted(jnp.cumsum(uneven_parts(own, LANGUAGE_COUNT, TOK_GROUP, RUN_MOST, 2)), jnp.arange(TOK_GROUP), side="right"))(jax.random.split(seeds[5], N_DP)).reshape((N_DP, TOK_GROUP)).astype(jnp.int32)
    owned = jax.random.permutation(seeds[6], LANGUAGE_COUNT).astype(jnp.int32)
    return {"hidden": hidden, "down_weight": down_weight, "adapter_first_factor": adapter_first_factor, "adapter_second_factor": adapter_second_factor, "output_gradient": output_gradient, "token_language_index": token_language_index, "owned": owned}


adapter_scale = 0.5


def select_language_rank(full, language_mask):
    rows = full.shape[0]
    return jnp.sum(full.reshape(rows, LANGUAGE_COUNT, ADAPTER_RANK) * language_mask[:, :, None], axis=1)


def spread_rank(small, language_mask):
    rows = small.shape[0]
    return (language_mask.astype(jnp.bfloat16)[:, :, None] * small.astype(jnp.bfloat16)[:, None, :]).reshape(rows, LANGUAGE_COUNT * ADAPTER_RANK)


def reference(hidden, down_weight, adapter_first_factor, adapter_second_factor, output_gradient, token_language_index, owned):
    labels = token_language_index.reshape(-1)
    language_mask = (labels[:, None] == jnp.arange(LANGUAGE_COUNT, dtype=jnp.int32)[None, :]).astype(jnp.float32)
    rank_reduce = select_language_rank(jnp.dot(hidden, adapter_first_factor, preferred_element_type=jnp.float32), language_mask)
    expanded_rank = spread_rank(rank_reduce, language_mask)
    frozen_output = jnp.dot(hidden, down_weight, preferred_element_type=jnp.float32)
    rank_expand = jnp.dot(expanded_rank, adapter_second_factor, preferred_element_type=jnp.float32)
    mixed = (frozen_output + adapter_scale * rank_expand).astype(jnp.bfloat16)
    input_gradient = select_language_rank(jnp.dot(output_gradient, adapter_second_factor.T, preferred_element_type=jnp.float32), language_mask)
    gradient_spread_rank = spread_rank(input_gradient, language_mask)
    hidden_gradient = (jnp.dot(output_gradient, down_weight.T, preferred_element_type=jnp.float32)
                   + adapter_scale * jnp.dot(gradient_spread_rank, adapter_first_factor.T, preferred_element_type=jnp.float32)).astype(jnp.bfloat16)
    complete_first_factor = adapter_scale * jnp.dot(gradient_spread_rank.T, hidden, preferred_element_type=jnp.float32)
    complete_second_factor = adapter_scale * jnp.dot(expanded_rank.T, output_gradient, preferred_element_type=jnp.float32)
    grad_a = jnp.take(complete_first_factor.reshape(LANGUAGE_COUNT, ADAPTER_RANK, HIDDEN_UNITS), owned, axis=0)
    grad_b = jnp.take(complete_second_factor.reshape(LANGUAGE_COUNT, ADAPTER_RANK, MODEL_WIDTH), owned, axis=0)
    return (mixed, hidden_gradient, grad_a, grad_b)
```

```python
import functools

import jax
import jax.numpy as jnp
from jax import lax
from jax.experimental import pallas as pl
from jax.experimental.pallas import tpu as pltpu
from jax.sharding import PartitionSpec as P

RANK = 16
LANGS = 64
WIDE = RANK * LANGS
LANES = 128
SCALE = 0.5
MESH = pl.DeviceIdType.MESH
BF16, F32 = jnp.bfloat16, jnp.float32


def nn(a, b):
    return jnp.dot(a, b, preferred_element_type=F32)


def nt(a, b):
    return lax.dot_general(a, b, (((1,), (1,)), ((), ())), preferred_element_type=F32)


def sizes_of(mesh, hidden, grad):
    nt_, ndp = mesh.shape["tensor"], mesh.shape["dp"]
    blocks = nt_ // 2
    features = grad.shape[1]
    return dict(
        nz=nt_ // 4,
        ny=ndp // 2,
        ndp=ndp,
        blocks=blocks,
        block=features // nt_,
        half=features // 2,
        rows=grad.shape[0],
        tokens=hidden.shape[0],
        units=hidden.shape[1],
        early=blocks * 7 // 16,
    )


def kernel(
    sz,
    hidden_ref, weight_ref, first_ref, second_ref, grad_ref, lab_col, lab_row, own_ref,
    mixed_out, hg_out, ga_out, gb_out,
    wk, hk, av, bv, gall, part, zr_p, zr_q, xr_q, xr_p, stage, mixbuf,
    ar_own, ar_quad, ar_z, ar_fin, sp_nat, sp_t, bk_nat, bk_t, lift,
    hg_own, hg_send, hg_recv, gb_part, ga_part, yr_b, yr_a, xs_b, xs_a, xr_b, xr_a,
    load_sem, swap_send, swap_recv,
    agz_s, agz_r, agp_s, agp_r, agq_s, agq_r,
    rsz_s, rsz_r, rsq_s, rsq_r, rsp_s, rsp_r, mix_s, mix_r,
    arq_s, arq_r, arz_s, arz_r, arf_s, arf_r,
    y_s, y_r, xh_s, xh_r, hg_s, hg_r,
):
    nz, ny, nb, fb, fh = sz["nz"], sz["ny"], sz["blocks"], sz["block"], sz["half"]
    rows, tokens, units = sz["rows"], sz["tokens"], sz["units"]
    quarter = tokens // 4
    own_rows = WIDE // sz["ndp"]
    pw = sz["early"] * fb
    pcols, qcols = slice(0, pw), slice(pw, fh)

    d, t = lax.axis_index("dp"), lax.axis_index("tensor")
    c, x, z, u = t % 2, (t // 2) % 2, t // 4, t % 4
    y, h = d % ny, d // ny
    jown = 2 * z + x

    core_dev = (d, t + 1 - 2 * c)
    x_dev = (d, t + 2 - 4 * x)
    quad_u = {1: u + 1 - 2 * c, 2: u + 2 - 4 * x, 3: 3 - u}

    def zwrap(v):
        return (v + 2 * nz) % nz

    def z_dev(k):
        return (d, zwrap(z + k) * 4 + u)

    def quad_dev(k):
        return (d, z * 4 + quad_u[k])

    def y_dev(k):
        return (h * ny + (y + k) % ny, t)

    h_dev = ((1 - h) * ny + y, t)

    def remote(src, dst, ssem, rsem, dev):
        return pltpu.make_async_remote_copy(
            src_ref=src, dst_ref=dst, send_sem=ssem, recv_sem=rsem, device_id=dev, device_id_type=MESH
        )

    def aligned(v, m):
        return pl.multiple_of(v, m)

    def slab(ref, zs, xs, cs, cols):
        return ref.at[pl.ds(aligned((zs * 4 + xs * 2 + cs) * rows, rows), rows), cols]

    def feat(j):
        return pl.ds(aligned(j * fb, fb), fb)

    def unit(k):
        return pl.ds(aligned(k * units, units), units)

    peers = [quad_dev(k) for k in (1, 2, 3)] + [z_dev(k) for k in range(1, nz)]
    peers += [y_dev(k) for k in range(1, ny)] + [h_dev]
    barrier = pltpu.get_barrier_semaphore()
    for peer in peers:
        pl.semaphore_signal(barrier, inc=1, device_id=peer, device_id_type=MESH)

    whole = slice(None)
    for j in range(nb):
        pltpu.make_async_copy(
            grad_ref.at[:, feat(2 * j + c)], slab(gall, z, x, c, pl.ds(j * fb, fb)), load_sem.at[0]
        ).start()
    load_h = pltpu.make_async_copy(hidden_ref, hk.at[:, unit(c)], load_sem.at[1])
    load_a = pltpu.make_async_copy(first_ref, av, load_sem.at[2])
    load_b = pltpu.make_async_copy(second_ref, bv, load_sem.at[3])
    load_h.start()
    load_a.start()
    pl.semaphore_wait(barrier, len(peers))

    for j in range(nb):
        remote(
            grad_ref.at[:, feat(2 * j + 1 - c)], slab(gall, z, x, c, pl.ds(j * fb, fb)),
            swap_send.at[0], swap_recv.at[0], core_dev,
        ).start()
    remote(hidden_ref, hk.at[:, unit(c)], swap_send.at[1], swap_recv.at[1], core_dev).start()
    for j in range(nb):
        pltpu.make_async_copy(
            weight_ref.at[:, feat(2 * j + c)], wk.at[unit(c), pl.ds(j * fb, fb)], load_sem.at[4]
        ).start()
        remote(
            weight_ref.at[:, feat(2 * j + 1 - c)], wk.at[unit(c), pl.ds(j * fb, fb)],
            swap_send.at[2], swap_recv.at[2], core_dev,
        ).start()
    load_b.start()

    def swap_wait(i):
        region = {
            0: lambda k: slab(gall, z, x, k, whole),
            1: lambda k: hk.at[:, unit(k)],
            2: lambda k: wk.at[unit(k), :],
        }[i]
        mine, theirs = region(c), region(1 - c)
        return (
            remote(theirs, theirs, swap_send.at[i], swap_recv.at[i], core_dev),
            remote(mine, mine, swap_send.at[i], swap_recv.at[i], core_dev),
        )

    def sign(way):
        return 1 - 2 * way

    chain_cols = (pcols, pcols, qcols)

    def chain_x(chain):
        return 1 - x if chain == 1 else x

    def ag_z(way, chain, s):
        ref = slab(gall, zwrap(z - sign(way) * s), chain_x(chain), way, chain_cols[chain])
        return remote(ref, ref, agz_s.at[way, chain, s], agz_r.at[way, chain, s], z_dev(sign(way)))

    def ag_z_in(way, chain, s):
        ref = slab(gall, zwrap(z - sign(way) * (s + 1)), chain_x(chain), way, chain_cols[chain])
        return remote(ref, ref, agz_s.at[way, chain, s], agz_r.at[way, chain, s], z_dev(sign(way)))

    def ag_p(way, xs):
        ref = slab(gall, z, xs, way, pcols)
        return remote(ref, ref, agp_s.at[way], agp_r.at[way], x_dev)

    def ag_q(way, k, xs):
        ref = slab(gall, zwrap(z - sign(way) * k), xs, way, qcols)
        return remote(ref, ref, agq_s.at[way, k], agq_r.at[way, k], x_dev)

    pltpu.make_async_copy(
        slab(gall, z, x, c, whole), slab(gall, z, x, c, whole), load_sem.at[0]
    ).wait()
    swap_wait(0)[0].wait_recv()
    for way in (0, 1):
        ag_p(way, x).start()
        ag_z(way, 0, 0).start()
        ag_z(way, 2, 0).start()
    for way in (0, 1):
        ag_q(way, 0, x).start()
    for way in (0, 1):
        ag_p(way, 1 - x).wait_recv()
        ag_z(way, 1, 0).start()

    def ag_step(s):
        for chain in (0, 2, 1):
            for way in (0, 1):
                ag_z_in(way, chain, s).wait_recv()
                if s + 1 < nz - 1:
                    ag_z(way, chain, s + 1).start()
                if chain == 2:
                    ag_q(way, s + 1, x).start()

    lane_lang = lax.broadcasted_iota(jnp.int32, (tokens, LANES), 1) // RANK
    per = LANES // RANK

    def pick(product, i):
        labels = jnp.broadcast_to(lab_col[...], (tokens, LANES))
        total = jnp.zeros((tokens, LANES), F32)
        step = 2 * LANES
        for g in range(WIDE // step):
            full = product(g * step, step)
            for k in range(2):
                lang = lane_lang + (2 * g + k) * per
                total += jnp.where(labels == lang, full[:, k * LANES : (k + 1) * LANES], 0.0)
        turned = total.T
        small = turned[:RANK]
        for g in range(1, per):
            small += turned[g * RANK : (g + 1) * RANK]
        for k in range(4):
            ar_own[i, k] = small[:, k * quarter : (k + 1) * quarter]

    def arq(i, k):
        return remote(ar_own.at[i, quad_u[k]], ar_quad.at[i, u], arq_s.at[i, k - 1], arq_r.at[i, k - 1], quad_dev(k))

    def arq_in(i, k):
        ref = ar_quad.at[i, quad_u[k]]
        return remote(ref, ref, arq_s.at[i, k - 1], arq_r.at[i, k - 1], quad_dev(k))

    def arz(i, k):
        ref = ar_z.at[i, z]
        return remote(ref, ref, arz_s.at[i, k - 1], arz_r.at[i, k - 1], z_dev(k))

    def arz_in(i, k):
        ref = ar_z.at[i, zwrap(z - k)]
        return remote(ref, ref, arz_s.at[i, k - 1], arz_r.at[i, k - 1], z_dev(k))

    def arf(i, k):
        ref = ar_fin.at[i, u]
        return remote(ref, ref, arf_s.at[i, k - 1], arf_r.at[i, k - 1], quad_dev(k))

    def arf_in(i, k):
        ref = ar_fin.at[i, quad_u[k]]
        return remote(ref, ref, arf_s.at[i, k - 1], arf_r.at[i, k - 1], quad_dev(k))

    def ar_first(i):
        for k in (3, 2, 1):
            arq(i, k).start()

    def ar_second(i):
        for k in (1, 2, 3):
            arq_in(i, k).wait_recv()
        total = ar_own[i, u]
        for k in (1, 2, 3):
            total += ar_quad[i, quad_u[k]]
        ar_z[i, z] = total
        for k in range(nz - 1, 0, -1):
            arz(i, k).start()

    def ar_third(i):
        for k in range(1, nz):
            arz_in(i, k).wait_recv()
        total = ar_z[i, 0]
        for k in range(1, nz):
            total += ar_z[i, k]
        ar_fin[i, u] = total
        for k in (3, 2, 1):
            arf(i, k).start()

    def ar_last(i, natural, turned):
        for k in (1, 2, 3):
            arf_in(i, k).wait_recv()
        small = jnp.concatenate([ar_fin[i, k] for k in range(4)], axis=1)
        languages = lab_row[...]
        for k in range(LANGS):
            turned[k * RANK : (k + 1) * RANK, :] = jnp.where(languages == own_ref[k], small, 0.0).astype(BF16)
        tall = jnp.concatenate([small] * per, axis=0).T
        labels = jnp.broadcast_to(lab_col[...], (tokens, LANES))
        for g in range(WIDE // LANES):
            natural[:, g * LANES : (g + 1) * LANES] = jnp.where(
                labels == lane_lang + g * per, tall, 0.0
            ).astype(BF16)

    def mix_blocks(lo, hi):
        def one(i, carry):
            cols = feat((jown + 1 + i) % nb)
            part[:, cols] = nn(hk[...], wk[:, cols]).astype(BF16)
            return carry

        if hi > lo:
            lax.fori_loop(lo, hi, one, 0)

    def mix_own():
        cols = feat(jown)
        part[:, cols] = (nn(hk[...], wk[:, cols]) + lift[...]).astype(BF16)

    load_h.wait()
    load_a.wait()
    h_own = hk[:, unit(c)]
    pick(lambda lo, n: nn(h_own, av[:, lo : lo + n]), 0)
    ar_first(0)

    splits = [(nb - 1) * s // (nz - 1) for s in range(nz)]
    for s in range(nz - 1):
        ag_step(s)
        if s == 0:
            ar_second(0)
            swap_wait(1)[0].wait_recv()
            swap_wait(2)[0].wait_recv()
            pltpu.make_async_copy(wk.at[unit(c), :], wk.at[unit(c), :], load_sem.at[4]).wait()
        if s == min(2, nz - 2):
            ar_third(0)
        if s == min(3, nz - 2):
            load_b.wait()
            ar_last(0, sp_nat, sp_t)
            lift[...] = SCALE * nn(sp_nat[...], bv[...])
        mix_blocks(splits[s], splits[s + 1])
    mix_own()

    def rs_z(way, chain, s):
        src = slab(part, zwrap(z - sign(way) * (s + 1)), chain_x(chain), way, chain_cols[chain])
        dst = zr_q.at[way, s] if chain == 2 else zr_p.at[way, s, chain]
        return remote(src, dst, rsz_s.at[way, chain, s], rsz_r.at[way, chain, s], z_dev(sign(way)))

    def rs_q(way, k):
        zs = zwrap(z - sign(way) * (k + 1))
        src = slab(part, zs, 1 - x, way, qcols)
        return remote(src, xr_q.at[zs, way], rsq_s.at[way, k], rsq_r.at[way, k], x_dev)

    def rs_p(way):
        src = slab(part, z, 1 - x, way, pcols)
        return remote(src, xr_p.at[way], rsp_s.at[way], rsp_r.at[way], x_dev)

    def rs_sum(way, chain, s):
        zs = zwrap(z - sign(way) * (s + 1))
        total = slab(part, zs, chain_x(chain), way, chain_cols[chain])[...].astype(F32)
        if chain == 2:
            rs_q(way, s).wait_recv()
            total += xr_q[zs, way].astype(F32)
        if s > 0:
            rs_z(way, chain, s - 1).wait_recv()
            got = zr_q[way, s - 1] if chain == 2 else zr_p[way, s - 1, chain]
            total += got.astype(F32)
        return total

    def rs_step(s):
        for chain in (1, 2, 0):
            for way in (0, 1):
                if s > 0 or chain == 2:
                    zs = zwrap(z - sign(way) * (s + 1))
                    slab(part, zs, chain_x(chain), way, chain_cols[chain])[...] = rs_sum(way, chain, s).astype(BF16)
                rs_z(way, chain, s).start()

    tile = min(256, units)
    mtile = tokens // 2
    ntiles = units // tile

    def hg_send_copy():
        return remote(hg_send, hg_recv, hg_s, hg_r, core_dev)

    def hg_piece(i):
        part_of, rest = i // (2 * ntiles), i % (2 * ntiles)
        n, m = rest // 2, rest % 2
        owner = c if part_of else 1 - c
        rows_of = pl.ds(aligned(owner * units + n * tile, tile), tile)
        value = nt(gall[m * mtile : (m + 1) * mtile, :], wk[rows_of, :])
        place = (slice(m * mtile, (m + 1) * mtile), slice(n * tile, (n + 1) * tile))
        if part_of:
            hg_own[place] = value
        else:
            hg_send[place] = value.astype(BF16)
        if i == 2 * ntiles - 1:
            hg_send_copy().start()

    pieces = list(range(4 * ntiles))

    def hg_some(count):
        for _ in range(min(count, len(pieces))):
            hg_piece(pieces.pop(0))

    def grads(turned, right, out):
        step = 256

        def one(i, carry):
            at = pl.ds(aligned(i * step, step), step)
            out[at, :] = (SCALE * nn(turned[at, :], right)).astype(BF16)
            return carry

        lax.fori_loop(0, WIDE // step, one, 0)

    sets = ((gb_part, yr_b, xs_b, xr_b, gb_out), (ga_part, yr_a, xs_a, xr_a, ga_out))

    def owner_rows(ref, hh, yy):
        return ref.at[pl.ds(aligned((hh * ny + yy) * own_rows, own_rows), own_rows), :]

    def y_copy(i, k, hh):
        src = owner_rows(sets[i][0], hh, (y + k) % ny)
        return remote(src, sets[i][1].at[k - 1, hh], y_s.at[i, k - 1, hh], y_r.at[i, k - 1, hh], y_dev(k))

    def y_send(i):
        for k in range(ny - 1, 0, -1):
            for hh in (0, 1):
                y_copy(i, k, hh).start()

    def y_total(i, hh):
        total = owner_rows(sets[i][0], hh, y)[...].astype(F32)
        for k in range(1, ny):
            total += sets[i][1][k - 1, hh].astype(F32)
        return total

    def h_copy(i):
        return remote(sets[i][2], sets[i][3], xh_s.at[i], xh_r.at[i], h_dev)

    def h_send(i):
        for k in range(1, ny):
            for hh in (0, 1):
                y_copy(i, k, hh).wait_recv()
        sets[i][2][...] = y_total(i, 1 - h).astype(BF16)
        h_copy(i).start()

    def h_last(i):
        total = y_total(i, h)
        h_copy(i).wait_recv()
        sets[i][4][...] = total + sets[i][3][...].astype(F32)

    for k in range(nz):
        for way in (0, 1):
            rs_q(way, k).start()
    for way in (0, 1):
        for chain in (1, 0):
            rs_z(way, chain, 0).start()
    for k in range(nz):
        for way in (0, 1):
            ag_q(way, k, 1 - x).wait_recv()
    g_block = gall[:, feat(jown)]
    pick(lambda lo, n: nt(g_block, bv[lo : lo + n, :]), 1)
    ar_first(1)
    for way in (0, 1):
        slab(part, zwrap(z - sign(way)), x, way, qcols)[...] = rs_sum(way, 2, 0).astype(BF16)
        rs_z(way, 2, 0).start()
    grads(sp_t, gall[:, feat(jown)], gb_part)
    y_send(0)
    ar_second(1)
    for s in range(1, nz - 1):
        rs_step(s)
        if s == 1:
            hg_some(2)
            ar_third(1)
        if s == min(2, nz - 2):
            ar_last(1, bk_nat, bk_t)
            grads(bk_t, hk[:, unit(c)], ga_part)
            y_send(1)
        if s > 2:
            hg_some(2)
        if s == min(4, nz - 2):
            h_send(0)
    hg_some(len(pieces))
    last = nz - 1
    for way in (0, 1):
        slab(part, z, 1 - x, way, pcols)[...] = rs_sum(way, 1, last).astype(BF16)
        rs_p(way).start()
    for way in (0, 1):
        stage[way, :, qcols] = rs_sum(way, 2, last).astype(BF16)
    h_send(1)
    for way in (0, 1):
        total = rs_sum(way, 0, last)
        rs_p(way).wait_recv()
        stage[way, :, pcols] = (total + xr_p[way].astype(F32)).astype(BF16)
    mix_copy = remote(stage.at[1 - c], mixbuf.at[c], mix_s, mix_r, core_dev)
    mix_copy.start()
    hg_send_copy().wait_recv()
    hg_out[...] = (hg_own[...] + hg_recv[...].astype(F32) + SCALE * nt(bk_nat[...], av[...])).astype(BF16)
    h_last(0)
    h_last(1)
    mixed_out[c] = stage[c]
    remote(stage.at[c], mixbuf.at[1 - c], mix_s, mix_r, core_dev).wait_recv()
    mixed_out[1 - c] = mixbuf[1 - c]

    for i in range(3):
        swap_wait(i)[1].wait_send()
    for way in (0, 1):
        ag_p(way, x).wait_send()
        rs_p(way).wait_send()
        for k in range(nz):
            ag_q(way, k, x).wait_send()
            rs_q(way, k).wait_send()
        for chain in range(3):
            for s in range(nz - 1):
                ag_z(way, chain, s).wait_send()
                rs_z(way, chain, s).wait_send()
    for i in range(2):
        for k in (1, 2, 3):
            arq(i, k).wait_send()
            arf(i, k).wait_send()
        for k in range(1, nz):
            arz(i, k).wait_send()
        for k in range(1, ny):
            for hh in (0, 1):
                y_copy(i, k, hh).wait_send()
        h_copy(i).wait_send()
    hg_send_copy().wait_send()
    mix_copy.wait_send()


def solution(mesh):
    def body(hidden, down_weight, first, second, grad, labels, owned):
        sz = sizes_of(mesh, hidden, grad)
        nz, ny, nb, fb, fh = sz["nz"], sz["ny"], sz["blocks"], sz["block"], sz["half"]
        rows, tokens, units = sz["rows"], sz["tokens"], sz["units"]
        quarter, own_rows = tokens // 4, WIDE // sz["ndp"]
        pw = sz["early"] * fb
        qw = fh - pw
        dma = pltpu.SemaphoreType.DMA
        vmem = pltpu.VMEM
        hop, kk = nz - 1, max(ny - 1, 1)
        scratch = [
            vmem((2 * units, fh), BF16),
            vmem((tokens, 2 * units), BF16),
            vmem((units, WIDE), BF16),
            vmem((WIDE, fb), BF16),
            vmem((tokens, fh), BF16),
            vmem((tokens, fh), BF16),
            vmem((2, hop, 2, rows, pw), BF16),
            vmem((2, hop, rows, qw), BF16),
            vmem((nz, 2, rows, qw), BF16),
            vmem((2, rows, pw), BF16),
            vmem((2, rows, fh), BF16),
            vmem((2, rows, fh), BF16),
            vmem((2, 4, RANK, quarter), F32),
            vmem((2, 4, RANK, quarter), F32),
            vmem((2, nz, RANK, quarter), F32),
            vmem((2, 4, RANK, quarter), F32),
            vmem((tokens, WIDE), BF16),
            vmem((WIDE, tokens), BF16),
            vmem((tokens, WIDE), BF16),
            vmem((WIDE, tokens), BF16),
            vmem((tokens, fb), F32),
            vmem((tokens, units), F32),
            vmem((tokens, units), BF16),
            vmem((tokens, units), BF16),
            vmem((WIDE, fb), BF16),
            vmem((WIDE, units), BF16),
            vmem((kk, 2, own_rows, fb), BF16),
            vmem((kk, 2, own_rows, units), BF16),
            vmem((own_rows, fb), BF16),
            vmem((own_rows, units), BF16),
            vmem((own_rows, fb), BF16),
            vmem((own_rows, units), BF16),
            dma((5,)), dma((3,)), dma((3,)),
            dma((2, 3, hop)), dma((2, 3, hop)), dma((2,)), dma((2,)), dma((2, nz)), dma((2, nz)),
            dma((2, 3, hop)), dma((2, 3, hop)), dma((2, nz)), dma((2, nz)), dma((2,)), dma((2,)), dma, dma,
            dma((2, 3)), dma((2, 3)), dma((2, hop)), dma((2, hop)), dma((2, 3)), dma((2, 3)),
            dma((2, kk, 2)), dma((2, kk, 2)), dma((2,)), dma((2,)), dma, dma,
        ]
        anywhere = pl.BlockSpec(memory_space=pl.ANY)
        on_chip = pl.BlockSpec(memory_space=pltpu.VMEM)
        mixed, hg, ga, gb = pl.pallas_call(
            functools.partial(kernel, sz),
            out_shape=(
                jax.ShapeDtypeStruct((2, rows, fh), BF16),
                jax.ShapeDtypeStruct((tokens, units), BF16),
                jax.ShapeDtypeStruct((own_rows, units), F32),
                jax.ShapeDtypeStruct((own_rows, fb), F32),
            ),
            in_specs=[anywhere] * 5 + [on_chip] * 2 + [pl.BlockSpec(memory_space=pltpu.SMEM)],
            out_specs=(on_chip,) * 4,
            scratch_shapes=scratch,
            compiler_params=pltpu.CompilerParams(
                collective_id=0, has_side_effects=True, vmem_limit_bytes=56 * 1024 * 1024
            ),
        )(hidden, down_weight, first, second, grad, labels.reshape(-1, 1), labels.reshape(1, -1), owned)
        mixed = mixed.reshape(2, rows, nb, fb).transpose(1, 2, 0, 3).reshape(rows, 2 * fh)
        slots = own_rows // RANK
        return mixed, hg, ga.reshape(slots, RANK, units), gb.reshape(slots, RANK, fb)

    in_specs = (
        P("dp", "tensor"),
        P("tensor", None),
        P("tensor", None),
        P(None, "tensor"),
        P(("dp", "tensor"), None),
        P("dp", None),
        P(),
    )
    out_specs = (
        P(("dp", "tensor"), None),
        P("dp", "tensor"),
        P("dp", None, "tensor"),
        P("dp", None, "tensor"),
    )
    return jax.shard_map(body, mesh=mesh, in_specs=in_specs, out_specs=out_specs, check_vma=False)
```

```python
import functools

import jax
import jax.numpy as jnp
from jax import lax
from jax.experimental import pallas as pl
from jax.experimental.pallas import tpu as pltpu
from jax.sharding import PartitionSpec as P

RANK = 16
LANGS = 64
WIDE = RANK * LANGS
LANES = 128
SCALE = 0.5
MESH = pl.DeviceIdType.MESH
BF16, F32 = jnp.bfloat16, jnp.float32


def nn(a, b):
    return jnp.dot(a, b, preferred_element_type=F32)


def nt(a, b):
    return lax.dot_general(a, b, (((1,), (1,)), ((), ())), preferred_element_type=F32)


def sizes_of(mesh, hidden, grad):
    nt_, ndp = mesh.shape["tensor"], mesh.shape["dp"]
    blocks = nt_ // 2
    features = grad.shape[1]
    return dict(
        nz=nt_ // 4,
        ny=ndp // 2,
        ndp=ndp,
        blocks=blocks,
        block=features // nt_,
        half=features // 2,
        rows=grad.shape[0],
        tokens=hidden.shape[0],
        units=hidden.shape[1],
        early=blocks * 7 // 16,
    )


def kernel(
    sz,
    hidden_ref, weight_ref, first_ref, second_ref, grad_ref, lab_row, own_ref,
    mixed_out, hg_out, ga_out, gb_out,
    wk, hk, av, bv, gall, part, zr_p, zr_q, xr_q, xr_p, stage, mixbuf,
    lab_col, ar_own, ar_quad, ar_z, ar_fin, sp_nat, sp_t, bk_nat, bk_t, lift,
    hg_own, hg_send, hg_recv, gb_part, ga_part, yr_b, yr_a, xs_b, xs_a, xr_b, xr_a,
    load_sem, swap_send, swap_recv,
    agz_s, agz_r, agp_s, agp_r, agq_s, agq_r,
    rsz_s, rsz_r, rsq_s, rsq_r, rsp_s, rsp_r, mix_s, mix_r,
    arq_s, arq_r, arz_s, arz_r, arf_s, arf_r,
    y_s, y_r, xh_s, xh_r, hg_s, hg_r,
):
    nz, ny, nb, fb, fh = sz["nz"], sz["ny"], sz["blocks"], sz["block"], sz["half"]
    rows, tokens, units = sz["rows"], sz["tokens"], sz["units"]
    quarter = tokens // 4
    own_rows = WIDE // sz["ndp"]
    pw = sz["early"] * fb
    pcols, qcols = slice(0, pw), slice(pw, fh)

    d, t = lax.axis_index("dp"), lax.axis_index("tensor")
    c, x, z, u = t % 2, (t // 2) % 2, t // 4, t % 4
    y, h = d % ny, d // ny
    jown = 2 * z + x

    core_dev = (d, t + 1 - 2 * c)
    x_dev = (d, t + 2 - 4 * x)
    quad_u = {1: u + 1 - 2 * c, 2: u + 2 - 4 * x, 3: 3 - u}

    def zwrap(v):
        return (v + 2 * nz) % nz

    def z_dev(k):
        return (d, zwrap(z + k) * 4 + u)

    def quad_dev(k):
        return (d, z * 4 + quad_u[k])

    def y_dev(k):
        return (h * ny + (y + k) % ny, t)

    h_dev = ((1 - h) * ny + y, t)

    def remote(src, dst, ssem, rsem, dev):
        return pltpu.make_async_remote_copy(
            src_ref=src, dst_ref=dst, send_sem=ssem, recv_sem=rsem, device_id=dev, device_id_type=MESH
        )

    def aligned(v, m):
        return pl.multiple_of(v, m)

    def slab(ref, zs, xs, cs, cols):
        return ref.at[pl.ds(aligned((zs * 4 + xs * 2 + cs) * rows, rows), rows), cols]

    def feat(j):
        return pl.ds(aligned(j * fb, fb), fb)

    def unit(k):
        return pl.ds(aligned(k * units, units), units)

    peers = [quad_dev(k) for k in (1, 2, 3)] + [z_dev(k) for k in range(1, nz)]
    peers += [y_dev(k) for k in range(1, ny)] + [h_dev]
    barrier = pltpu.get_barrier_semaphore()
    for peer in peers:
        pl.semaphore_signal(barrier, inc=1, device_id=peer, device_id_type=MESH)

    whole = slice(None)
    for j in range(nb):
        pltpu.make_async_copy(
            grad_ref.at[:, feat(2 * j + c)], slab(gall, z, x, c, pl.ds(j * fb, fb)), load_sem.at[0]
        ).start()
    load_h = pltpu.make_async_copy(hidden_ref, hk.at[:, unit(c)], load_sem.at[1])
    load_a = pltpu.make_async_copy(first_ref, av, load_sem.at[2])
    load_b = pltpu.make_async_copy(second_ref, bv, load_sem.at[3])
    load_h.start()
    load_a.start()
    lab_col[...] = jnp.broadcast_to(lab_row[...], (LANES, tokens)).T
    pl.semaphore_wait(barrier, len(peers))

    for j in range(nb):
        remote(
            grad_ref.at[:, feat(2 * j + 1 - c)], slab(gall, z, x, c, pl.ds(j * fb, fb)),
            swap_send.at[0], swap_recv.at[0], core_dev,
        ).start()
    remote(hidden_ref, hk.at[:, unit(c)], swap_send.at[1], swap_recv.at[1], core_dev).start()
    for j in range(nb):
        pltpu.make_async_copy(
            weight_ref.at[:, feat(2 * j + c)], wk.at[unit(c), pl.ds(j * fb, fb)], load_sem.at[4]
        ).start()
        remote(
            weight_ref.at[:, feat(2 * j + 1 - c)], wk.at[unit(c), pl.ds(j * fb, fb)],
            swap_send.at[2], swap_recv.at[2], core_dev,
        ).start()
    load_b.start()

    def swap_wait(i):
        region = {
            0: lambda k: slab(gall, z, x, k, whole),
            1: lambda k: hk.at[:, unit(k)],
            2: lambda k: wk.at[unit(k), :],
        }[i]
        mine, theirs = region(c), region(1 - c)
        return (
            remote(theirs, theirs, swap_send.at[i], swap_recv.at[i], core_dev),
            remote(mine, mine, swap_send.at[i], swap_recv.at[i], core_dev),
        )

    def sign(way):
        return 1 - 2 * way

    chain_cols = (pcols, pcols, qcols)

    def chain_x(chain):
        return 1 - x if chain == 1 else x

    def ag_z(way, chain, s):
        ref = slab(gall, zwrap(z - sign(way) * s), chain_x(chain), way, chain_cols[chain])
        return remote(ref, ref, agz_s.at[way, chain, s], agz_r.at[way, chain, s], z_dev(sign(way)))

    def ag_z_in(way, chain, s):
        ref = slab(gall, zwrap(z - sign(way) * (s + 1)), chain_x(chain), way, chain_cols[chain])
        return remote(ref, ref, agz_s.at[way, chain, s], agz_r.at[way, chain, s], z_dev(sign(way)))

    def ag_p(way, xs):
        ref = slab(gall, z, xs, way, pcols)
        return remote(ref, ref, agp_s.at[way], agp_r.at[way], x_dev)

    def ag_q(way, k, xs):
        ref = slab(gall, zwrap(z - sign(way) * k), xs, way, qcols)
        return remote(ref, ref, agq_s.at[way, k], agq_r.at[way, k], x_dev)

    pltpu.make_async_copy(
        slab(gall, z, x, c, whole), slab(gall, z, x, c, whole), load_sem.at[0]
    ).wait()
    swap_wait(0)[0].wait_recv()
    for way in (0, 1):
        ag_p(way, x).start()
        ag_z(way, 0, 0).start()
        ag_z(way, 2, 0).start()
    for way in (0, 1):
        ag_q(way, 0, x).start()
    for way in (0, 1):
        ag_p(way, 1 - x).wait_recv()
        ag_z(way, 1, 0).start()

    def ag_step(s):
        for chain in (0, 2, 1):
            for way in (0, 1):
                ag_z_in(way, chain, s).wait_recv()
                if s + 1 < nz - 1:
                    ag_z(way, chain, s + 1).start()
                if chain == 2:
                    ag_q(way, s + 1, x).start()

    lane_lang = lax.broadcasted_iota(jnp.int32, (tokens, LANES), 1) // RANK
    per = LANES // RANK

    def pick(product, i):
        labels = lab_col[...]
        total = jnp.zeros((tokens, LANES), F32)
        step = 2 * LANES
        for g in range(WIDE // step):
            full = product(g * step, step)
            for k in range(2):
                lang = lane_lang + (2 * g + k) * per
                total += jnp.where(labels == lang, full[:, k * LANES : (k + 1) * LANES], 0.0)
        turned = total.T
        small = turned[:RANK]
        for g in range(1, per):
            small += turned[g * RANK : (g + 1) * RANK]
        for k in range(4):
            ar_own[i, k] = small[:, k * quarter : (k + 1) * quarter]

    def arq(i, k):
        return remote(ar_own.at[i, quad_u[k]], ar_quad.at[i, u], arq_s.at[i, k - 1], arq_r.at[i, k - 1], quad_dev(k))

    def arq_in(i, k):
        ref = ar_quad.at[i, quad_u[k]]
        return remote(ref, ref, arq_s.at[i, k - 1], arq_r.at[i, k - 1], quad_dev(k))

    def arz(i, k):
        ref = ar_z.at[i, z]
        return remote(ref, ref, arz_s.at[i, k - 1], arz_r.at[i, k - 1], z_dev(k))

    def arz_in(i, k):
        ref = ar_z.at[i, zwrap(z - k)]
        return remote(ref, ref, arz_s.at[i, k - 1], arz_r.at[i, k - 1], z_dev(k))

    def arf(i, k):
        ref = ar_fin.at[i, u]
        return remote(ref, ref, arf_s.at[i, k - 1], arf_r.at[i, k - 1], quad_dev(k))

    def arf_in(i, k):
        ref = ar_fin.at[i, quad_u[k]]
        return remote(ref, ref, arf_s.at[i, k - 1], arf_r.at[i, k - 1], quad_dev(k))

    def ar_first(i):
        for k in (3, 2, 1):
            arq(i, k).start()

    def ar_second(i):
        for k in (1, 2, 3):
            arq_in(i, k).wait_recv()
        total = ar_own[i, u]
        for k in (1, 2, 3):
            total += ar_quad[i, quad_u[k]]
        ar_z[i, z] = total
        for k in range(nz - 1, 0, -1):
            arz(i, k).start()

    def ar_third(i):
        for k in range(1, nz):
            arz_in(i, k).wait_recv()
        total = ar_z[i, 0]
        for k in range(1, nz):
            total += ar_z[i, k]
        ar_fin[i, u] = total
        for k in (3, 2, 1):
            arf(i, k).start()

    def ar_last(i, natural, turned):
        for k in (1, 2, 3):
            arf_in(i, k).wait_recv()
        small = jnp.concatenate([ar_fin[i, k] for k in range(4)], axis=1)
        languages = lab_row[...]
        for k in range(LANGS):
            turned[k * RANK : (k + 1) * RANK, :] = jnp.where(languages == own_ref[k], small, 0.0).astype(BF16)
        tall = jnp.concatenate([small] * per, axis=0).T
        labels = lab_col[...]
        for g in range(WIDE // LANES):
            natural[:, g * LANES : (g + 1) * LANES] = jnp.where(
                labels == lane_lang + g * per, tall, 0.0
            ).astype(BF16)

    def mix_blocks(lo, hi):
        def one(i, carry):
            cols = feat((jown + 1 + i) % nb)
            part[:, cols] = nn(hk[...], wk[:, cols]).astype(BF16)
            return carry

        if hi > lo:
            lax.fori_loop(lo, hi, one, 0)

    def mix_own():
        cols = feat(jown)
        part[:, cols] = (nn(hk[...], wk[:, cols]) + lift[...]).astype(BF16)

    load_h.wait()
    load_a.wait()
    h_own = hk[:, unit(c)]
    pick(lambda lo, n: nn(h_own, av[:, lo : lo + n]), 0)
    ar_first(0)

    def rs_z(way, chain, s):
        src = slab(part, zwrap(z - sign(way) * (s + 1)), chain_x(chain), way, chain_cols[chain])
        dst = zr_q.at[way, s] if chain == 2 else zr_p.at[way, s, chain]
        return remote(src, dst, rsz_s.at[way, chain, s], rsz_r.at[way, chain, s], z_dev(sign(way)))

    def rs_q(way, k):
        zs = zwrap(z - sign(way) * (k + 1))
        src = slab(part, zs, 1 - x, way, qcols)
        return remote(src, xr_q.at[zs, way], rsq_s.at[way, k], rsq_r.at[way, k], x_dev)

    def rs_p(way):
        src = slab(part, z, 1 - x, way, pcols)
        return remote(src, xr_p.at[way], rsp_s.at[way], rsp_r.at[way], x_dev)

    def rs_sum(way, chain, s):
        zs = zwrap(z - sign(way) * (s + 1))
        total = slab(part, zs, chain_x(chain), way, chain_cols[chain])[...].astype(F32)
        if chain == 2:
            rs_q(way, s).wait_recv()
            total += xr_q[zs, way].astype(F32)
        if s > 0:
            rs_z(way, chain, s - 1).wait_recv()
            got = zr_q[way, s - 1] if chain == 2 else zr_p[way, s - 1, chain]
            total += got.astype(F32)
        return total

    def rs_ahead(k):
        if k < nz:
            for way in (0, 1):
                rs_q(way, k).start()

    def rs_step(s):
        rs_ahead(s + 2)
        for chain in (1, 2, 0):
            for way in (0, 1):
                if s > 0 or chain == 2:
                    zs = zwrap(z - sign(way) * (s + 1))
                    slab(part, zs, chain_x(chain), way, chain_cols[chain])[...] = rs_sum(way, chain, s).astype(BF16)
                rs_z(way, chain, s).start()

    first_mix = min(1, nz - 2)
    last_mix = max(nz - 3, first_mix)
    spans = last_mix - first_mix + 1
    splits = [(nb - 1) * n // spans for n in range(spans + 1)]

    def shrink_done():
        ar_last(0, sp_nat, sp_t)
        lift[...] = SCALE * nn(sp_nat[...], bv[...])

    for s in range(nz - 2):
        ag_step(s)
        if s == 0:
            ar_second(0)
        if s == first_mix:
            swap_wait(1)[0].wait_recv()
            swap_wait(2)[0].wait_recv()
            pltpu.make_async_copy(wk.at[unit(c), :], wk.at[unit(c), :], load_sem.at[4]).wait()
            load_b.wait()
        if s == min(3, last_mix):
            ar_third(0)
        if s == last_mix:
            shrink_done()
        if s >= first_mix:
            mix_blocks(splits[s - first_mix], splits[s - first_mix + 1])
    mix_own()
    for way in (0, 1):
        for chain in (1, 0):
            rs_z(way, chain, 0).start()
    ag_step(nz - 2)
    for k in (0, 1):
        for way in (0, 1):
            rs_q(way, k).start()

    tile = min(256, units)
    mtile = tokens // 2
    ntiles = units // tile

    def hg_send_copy():
        return remote(hg_send, hg_recv, hg_s, hg_r, core_dev)

    def hg_piece(i):
        part_of, rest = i // (2 * ntiles), i % (2 * ntiles)
        n, m = rest // 2, rest % 2
        owner = c if part_of else 1 - c
        rows_of = pl.ds(aligned(owner * units + n * tile, tile), tile)
        value = nt(gall[m * mtile : (m + 1) * mtile, :], wk[rows_of, :])
        place = (slice(m * mtile, (m + 1) * mtile), slice(n * tile, (n + 1) * tile))
        if part_of:
            hg_own[place] = value
        else:
            hg_send[place] = value.astype(BF16)
        if i == 2 * ntiles - 1:
            hg_send_copy().start()

    pieces = list(range(4 * ntiles))

    def hg_some(count):
        for _ in range(min(count, len(pieces))):
            hg_piece(pieces.pop(0))

    def grads(turned, right, out):
        step = 256

        def one(i, carry):
            at = pl.ds(aligned(i * step, step), step)
            out[at, :] = (SCALE * nn(turned[at, :], right)).astype(BF16)
            return carry

        lax.fori_loop(0, WIDE // step, one, 0)

    sets = ((gb_part, yr_b, xs_b, xr_b, gb_out), (ga_part, yr_a, xs_a, xr_a, ga_out))

    def owner_rows(ref, hh, yy):
        return ref.at[pl.ds(aligned((hh * ny + yy) * own_rows, own_rows), own_rows), :]

    def y_hop(k, hh):
        return k if k in (1, ny - 1) else (ny - 1 if hh else 1)

    relayed = ((1, 0), (3, 1)) if ny == 4 else ()

    def y_copy(i, k, hh):
        src = owner_rows(sets[i][0], hh, (y + k) % ny)
        return remote(src, sets[i][1].at[k - 1, hh], y_s.at[i, k - 1, hh], y_r.at[i, k - 1, hh], y_dev(y_hop(k, hh)))

    def y_send(i):
        for k in (2, 1, 3) if ny == 4 else range(1, ny):
            for hh in (0, 1):
                if (k, hh) not in relayed:
                    y_copy(i, k, hh).start()

    def y_mid(i):
        for k, hh in relayed:
            y_copy(i, 2, hh).wait_recv()
            mine = owner_rows(sets[i][0], hh, (y + k) % ny)
            mine[...] = (mine[...].astype(F32) + sets[i][1][1, hh].astype(F32)).astype(BF16)
            y_copy(i, k, hh).start()

    y_direct = (1, 3) if ny == 4 else tuple(range(1, ny))

    def y_total(i, hh):
        total = owner_rows(sets[i][0], hh, y)[...].astype(F32)
        for k in y_direct:
            total += sets[i][1][k - 1, hh].astype(F32)
        return total

    def h_copy(i):
        return remote(sets[i][2], sets[i][3], xh_s.at[i], xh_r.at[i], h_dev)

    def h_send(i):
        for k in y_direct:
            for hh in (0, 1):
                y_copy(i, k, hh).wait_recv()
        sets[i][2][...] = y_total(i, 1 - h).astype(BF16)
        h_copy(i).start()

    def h_last(i):
        total = y_total(i, h)
        h_copy(i).wait_recv()
        sets[i][4][...] = total + sets[i][3][...].astype(F32)

    for k in range(nz):
        for way in (0, 1):
            ag_q(way, k, 1 - x).wait_recv()
    g_block = gall[:, feat(jown)]
    pick(lambda lo, n: nt(g_block, bv[lo : lo + n, :]), 1)
    ar_first(1)
    for way in (0, 1):
        slab(part, zwrap(z - sign(way)), x, way, qcols)[...] = rs_sum(way, 2, 0).astype(BF16)
        rs_z(way, 2, 0).start()
    rs_ahead(2)
    grads(sp_t, gall[:, feat(jown)], gb_part)
    y_send(0)
    at = {name: min(s, nz - 2) for name, s in dict(second=1, mid_b=2, third=3, back=4, h_b=5, mid_a=6).items()}
    for s in range(1, nz - 1):
        rs_step(s)
        if s == at["second"]:
            ar_second(1)
        if s == at["mid_b"]:
            y_mid(0)
        if s == at["third"]:
            ar_third(1)
        if s == at["back"]:
            ar_last(1, bk_nat, bk_t)
            grads(bk_t, hk[:, unit(c)], ga_part)
            y_send(1)
        else:
            hg_some(2)
        if s == at["h_b"]:
            h_send(0)
        if s == at["mid_a"]:
            y_mid(1)
    hg_some(len(pieces))
    last = nz - 1
    for way in (0, 1):
        slab(part, z, 1 - x, way, pcols)[...] = rs_sum(way, 1, last).astype(BF16)
        rs_p(way).start()
    for way in (0, 1):
        stage[way, :, qcols] = rs_sum(way, 2, last).astype(BF16)
    h_send(1)
    for way in (0, 1):
        total = rs_sum(way, 0, last)
        rs_p(way).wait_recv()
        stage[way, :, pcols] = (total + xr_p[way].astype(F32)).astype(BF16)
    mix_copy = remote(stage.at[1 - c], mixbuf.at[c], mix_s, mix_r, core_dev)
    mix_copy.start()
    hg_send_copy().wait_recv()
    hg_out[...] = (hg_own[...] + hg_recv[...].astype(F32) + SCALE * nt(bk_nat[...], av[...])).astype(BF16)
    h_last(0)
    h_last(1)
    for j in range(nb):
        mixed_out[:, feat(2 * j + c)] = stage[c, :, j * fb : (j + 1) * fb]
    remote(stage.at[c], mixbuf.at[1 - c], mix_s, mix_r, core_dev).wait_recv()
    for j in range(nb):
        mixed_out[:, feat(2 * j + 1 - c)] = mixbuf[1 - c, :, j * fb : (j + 1) * fb]

    for i in range(3):
        swap_wait(i)[1].wait_send()
    for way in (0, 1):
        ag_p(way, x).wait_send()
        rs_p(way).wait_send()
        for k in range(nz):
            ag_q(way, k, x).wait_send()
            rs_q(way, k).wait_send()
        for chain in range(3):
            for s in range(nz - 1):
                ag_z(way, chain, s).wait_send()
                rs_z(way, chain, s).wait_send()
    for i in range(2):
        for k in (1, 2, 3):
            arq(i, k).wait_send()
            arf(i, k).wait_send()
        for k in range(1, nz):
            arz(i, k).wait_send()
        for k in range(1, ny):
            for hh in (0, 1):
                y_copy(i, k, hh).wait_send()
        h_copy(i).wait_send()
    hg_send_copy().wait_send()
    mix_copy.wait_send()


def solution(mesh):
    def body(hidden, down_weight, first, second, grad, labels, owned):
        sz = sizes_of(mesh, hidden, grad)
        nz, ny, nb, fb, fh = sz["nz"], sz["ny"], sz["blocks"], sz["block"], sz["half"]
        rows, tokens, units = sz["rows"], sz["tokens"], sz["units"]
        quarter, own_rows = tokens // 4, WIDE // sz["ndp"]
        pw = sz["early"] * fb
        qw = fh - pw
        dma = pltpu.SemaphoreType.DMA
        vmem = pltpu.VMEM
        hop, kk = nz - 1, max(ny - 1, 1)
        scratch = [
            vmem((2 * units, fh), BF16),
            vmem((tokens, 2 * units), BF16),
            vmem((units, WIDE), BF16),
            vmem((WIDE, fb), BF16),
            vmem((tokens, fh), BF16),
            vmem((tokens, fh), BF16),
            vmem((2, hop, 2, rows, pw), BF16),
            vmem((2, hop, rows, qw), BF16),
            vmem((nz, 2, rows, qw), BF16),
            vmem((2, rows, pw), BF16),
            vmem((2, rows, fh), BF16),
            vmem((2, rows, fh), BF16),
            vmem((tokens, LANES), jnp.int32),
            vmem((2, 4, RANK, quarter), F32),
            vmem((2, 4, RANK, quarter), F32),
            vmem((2, nz, RANK, quarter), F32),
            vmem((2, 4, RANK, quarter), F32),
            vmem((tokens, WIDE), BF16),
            vmem((WIDE, tokens), BF16),
            vmem((tokens, WIDE), BF16),
            vmem((WIDE, tokens), BF16),
            vmem((tokens, fb), F32),
            vmem((tokens, units), F32),
            vmem((tokens, units), BF16),
            vmem((tokens, units), BF16),
            vmem((WIDE, fb), BF16),
            vmem((WIDE, units), BF16),
            vmem((kk, 2, own_rows, fb), BF16),
            vmem((kk, 2, own_rows, units), BF16),
            vmem((own_rows, fb), BF16),
            vmem((own_rows, units), BF16),
            vmem((own_rows, fb), BF16),
            vmem((own_rows, units), BF16),
            dma((5,)), dma((3,)), dma((3,)),
            dma((2, 3, hop)), dma((2, 3, hop)), dma((2,)), dma((2,)), dma((2, nz)), dma((2, nz)),
            dma((2, 3, hop)), dma((2, 3, hop)), dma((2, nz)), dma((2, nz)), dma((2,)), dma((2,)), dma, dma,
            dma((2, 3)), dma((2, 3)), dma((2, hop)), dma((2, hop)), dma((2, 3)), dma((2, 3)),
            dma((2, kk, 2)), dma((2, kk, 2)), dma((2,)), dma((2,)), dma, dma,
        ]
        anywhere = pl.BlockSpec(memory_space=pl.ANY)
        on_chip = pl.BlockSpec(memory_space=pltpu.VMEM)
        mixed, hg, ga, gb = pl.pallas_call(
            functools.partial(kernel, sz),
            out_shape=(
                jax.ShapeDtypeStruct((rows, 2 * fh), BF16),
                jax.ShapeDtypeStruct((tokens, units), BF16),
                jax.ShapeDtypeStruct((own_rows, units), F32),
                jax.ShapeDtypeStruct((own_rows, fb), F32),
            ),
            in_specs=[anywhere] * 5 + [on_chip] + [pl.BlockSpec(memory_space=pltpu.SMEM)],
            out_specs=(on_chip,) * 4,
            scratch_shapes=scratch,
            compiler_params=pltpu.CompilerParams(
                collective_id=0, has_side_effects=True, vmem_limit_bytes=56 * 1024 * 1024
            ),
        )(hidden, down_weight, first, second, grad, labels, owned)
        slots = own_rows // RANK
        return mixed, hg, ga.reshape(slots, RANK, units), gb.reshape(slots, RANK, fb)

    in_specs = (
        P("dp", "tensor"),
        P("tensor", None),
        P("tensor", None),
        P(None, "tensor"),
        P(("dp", "tensor"), None),
        P("dp", None),
        P(),
    )
    out_specs = (
        P(("dp", "tensor"), None),
        P("dp", "tensor"),
        P("dp", None, "tensor"),
        P("dp", None, "tensor"),
    )
    return jax.shard_map(body, mesh=mesh, in_specs=in_specs, out_specs=out_specs, check_vma=False)
```

```python
import functools

import jax
import jax.numpy as jnp
from jax import lax
from jax.experimental import pallas as pl
from jax.experimental.pallas import tpu as pltpu
from jax.sharding import PartitionSpec as P

RANK = 16
LANGS = 64
WIDE = RANK * LANGS
LANES = 128
SCALE = 0.5
MESH = pl.DeviceIdType.MESH
BF16, F32 = jnp.bfloat16, jnp.float32


def nn(a, b):
    return jnp.dot(a, b, preferred_element_type=F32)


def nt(a, b):
    return lax.dot_general(a, b, (((1,), (1,)), ((), ())), preferred_element_type=F32)


def sizes_of(mesh, hidden, grad):
    nt_, ndp = mesh.shape["tensor"], mesh.shape["dp"]
    blocks = nt_ // 2
    features = grad.shape[1]
    return dict(
        nz=nt_ // 4,
        ny=ndp // 2,
        ndp=ndp,
        blocks=blocks,
        block=features // nt_,
        half=features // 2,
        rows=grad.shape[0],
        tokens=hidden.shape[0],
        units=hidden.shape[1],
        early=blocks * 6 // 16,
    )


def kernel(
    sz,
    hidden_ref, weight_ref, first_ref, second_ref, grad_ref, lab_row, own_ref,
    mixed_out, hg_out, ga_out, gb_out,
    wk, hk, av, bv, gall, part, zr_p, zr_q, xr_q, xr_p, stage, mixbuf,
    lab_col, ar_own, ar_quad, ar_z, ar_fin, sp_nat, sp_t, bk_nat, bk_t, lift,
    hg_own, hg_send, hg_recv, gb_part, ga_part, yr_b, yr_a, xs_b, xs_a, xr_b, xr_a,
    load_sem, swap_send, swap_recv,
    agz_s, agz_r, agp_s, agp_r, agq_s, agq_r,
    rsz_s, rsz_r, rsq_s, rsq_r, rsp_s, rsp_r, mix_s, mix_r,
    arq_s, arq_r, arz_s, arz_r, arf_s, arf_r,
    y_s, y_r, xh_s, xh_r, hg_s, hg_r,
):
    nz, ny, nb, fb, fh = sz["nz"], sz["ny"], sz["blocks"], sz["block"], sz["half"]
    rows, tokens, units = sz["rows"], sz["tokens"], sz["units"]
    quarter = tokens // 4
    own_rows = WIDE // sz["ndp"]
    pw = sz["early"] * fb
    pcols, qcols = slice(0, pw), slice(pw, fh)

    d, t = lax.axis_index("dp"), lax.axis_index("tensor")
    c, x, z, u = t % 2, (t // 2) % 2, t // 4, t % 4
    y, h = d % ny, d // ny
    jown = 2 * z + x

    core_dev = (d, t + 1 - 2 * c)
    x_dev = (d, t + 2 - 4 * x)
    quad_u = {1: u + 1 - 2 * c, 2: u + 2 - 4 * x, 3: 3 - u}

    def zwrap(v):
        return (v + 2 * nz) % nz

    def z_dev(k):
        return (d, zwrap(z + k) * 4 + u)

    def quad_dev(k):
        return (d, z * 4 + quad_u[k])

    def y_dev(k):
        return (h * ny + (y + k) % ny, t)

    h_dev = ((1 - h) * ny + y, t)

    def remote(src, dst, ssem, rsem, dev):
        return pltpu.make_async_remote_copy(
            src_ref=src, dst_ref=dst, send_sem=ssem, recv_sem=rsem, device_id=dev, device_id_type=MESH
        )

    def aligned(v, m):
        return pl.multiple_of(v, m)

    def slab(ref, zs, xs, cs, cols):
        return ref.at[pl.ds(aligned((zs * 4 + xs * 2 + cs) * rows, rows), rows), cols]

    def feat(j):
        return pl.ds(aligned(j * fb, fb), fb)

    def unit(k):
        return pl.ds(aligned(k * units, units), units)

    peers = [quad_dev(k) for k in (1, 2, 3)] + [z_dev(k) for k in range(1, nz)]
    peers += [y_dev(k) for k in range(1, ny)] + [h_dev]
    barrier = pltpu.get_barrier_semaphore()
    for peer in peers:
        pl.semaphore_signal(barrier, inc=1, device_id=peer, device_id_type=MESH)

    whole = slice(None)
    for j in range(nb):
        pltpu.make_async_copy(
            grad_ref.at[:, feat(2 * j + c)], slab(gall, z, x, c, pl.ds(j * fb, fb)), load_sem.at[0]
        ).start()
    load_h = pltpu.make_async_copy(hidden_ref, hk.at[:, unit(c)], load_sem.at[1])
    load_a = pltpu.make_async_copy(first_ref, av, load_sem.at[2])
    load_b = pltpu.make_async_copy(second_ref, bv, load_sem.at[3])
    load_h.start()
    load_a.start()
    lab_col[...] = jnp.broadcast_to(lab_row[...], (LANES, tokens)).T
    pl.semaphore_wait(barrier, len(peers))

    for j in range(nb):
        remote(
            grad_ref.at[:, feat(2 * j + 1 - c)], slab(gall, z, x, c, pl.ds(j * fb, fb)),
            swap_send.at[0], swap_recv.at[0], core_dev,
        ).start()
    remote(hidden_ref, hk.at[:, unit(c)], swap_send.at[1], swap_recv.at[1], core_dev).start()
    for j in range(nb):
        pltpu.make_async_copy(
            weight_ref.at[:, feat(2 * j + c)], wk.at[unit(c), pl.ds(j * fb, fb)], load_sem.at[4]
        ).start()
        remote(
            weight_ref.at[:, feat(2 * j + 1 - c)], wk.at[unit(c), pl.ds(j * fb, fb)],
            swap_send.at[2], swap_recv.at[2], core_dev,
        ).start()
    load_b.start()

    def swap_wait(i):
        region = {
            0: lambda k: slab(gall, z, x, k, whole),
            1: lambda k: hk.at[:, unit(k)],
            2: lambda k: wk.at[unit(k), :],
        }[i]
        mine, theirs = region(c), region(1 - c)
        return (
            remote(theirs, theirs, swap_send.at[i], swap_recv.at[i], core_dev),
            remote(mine, mine, swap_send.at[i], swap_recv.at[i], core_dev),
        )

    def sign(way):
        return 1 - 2 * way

    chain_cols = (pcols, pcols, qcols)

    def chain_x(chain):
        return 1 - x if chain == 1 else x

    def ag_z(way, chain, s):
        ref = slab(gall, zwrap(z - sign(way) * s), chain_x(chain), way, chain_cols[chain])
        return remote(ref, ref, agz_s.at[way, chain, s], agz_r.at[way, chain, s], z_dev(sign(way)))

    def ag_z_in(way, chain, s):
        ref = slab(gall, zwrap(z - sign(way) * (s + 1)), chain_x(chain), way, chain_cols[chain])
        return remote(ref, ref, agz_s.at[way, chain, s], agz_r.at[way, chain, s], z_dev(sign(way)))

    def ag_p(way, xs):
        ref = slab(gall, z, xs, way, pcols)
        return remote(ref, ref, agp_s.at[way], agp_r.at[way], x_dev)

    def ag_q(way, k, xs):
        ref = slab(gall, zwrap(z - sign(way) * k), xs, way, qcols)
        return remote(ref, ref, agq_s.at[way, k], agq_r.at[way, k], x_dev)

    pltpu.make_async_copy(
        slab(gall, z, x, c, whole), slab(gall, z, x, c, whole), load_sem.at[0]
    ).wait()
    for way in (c, 1 - c):
        if way is not c:
            swap_wait(0)[0].wait_recv()
        ag_p(way, x).start()
        ag_z(way, 0, 0).start()
        ag_z(way, 2, 0).start()
    for way in (0, 1):
        ag_q(way, 0, x).start()
    for way in (0, 1):
        ag_p(way, 1 - x).wait_recv()
        ag_z(way, 1, 0).start()

    def ag_step(s):
        for chain in (0, 2, 1):
            for way in (0, 1):
                ag_z_in(way, chain, s).wait_recv()
                if s + 1 < nz - 1:
                    ag_z(way, chain, s + 1).start()
                if chain == 2:
                    ag_q(way, s + 1, x).start()

    lane_lang = lax.broadcasted_iota(jnp.int32, (tokens, LANES), 1) // RANK
    per = LANES // RANK

    def pick(product, i):
        labels = lab_col[...]
        total = jnp.zeros((tokens, LANES), F32)
        step = 2 * LANES
        for g in range(WIDE // step):
            full = product(g * step, step)
            for k in range(2):
                lang = lane_lang + (2 * g + k) * per
                total += jnp.where(labels == lang, full[:, k * LANES : (k + 1) * LANES], 0.0)
        turned = total.T
        small = turned[:RANK]
        for g in range(1, per):
            small += turned[g * RANK : (g + 1) * RANK]
        for k in range(4):
            ar_own[i, k] = small[:, k * quarter : (k + 1) * quarter]

    def arq(i, k):
        return remote(ar_own.at[i, quad_u[k]], ar_quad.at[i, u], arq_s.at[i, k - 1], arq_r.at[i, k - 1], quad_dev(k))

    def arq_in(i, k):
        ref = ar_quad.at[i, quad_u[k]]
        return remote(ref, ref, arq_s.at[i, k - 1], arq_r.at[i, k - 1], quad_dev(k))

    def arz(i, k):
        ref = ar_z.at[i, z]
        return remote(ref, ref, arz_s.at[i, k - 1], arz_r.at[i, k - 1], z_dev(k))

    def arz_in(i, k):
        ref = ar_z.at[i, zwrap(z - k)]
        return remote(ref, ref, arz_s.at[i, k - 1], arz_r.at[i, k - 1], z_dev(k))

    def arf(i, k):
        ref = ar_fin.at[i, u]
        return remote(ref, ref, arf_s.at[i, k - 1], arf_r.at[i, k - 1], quad_dev(k))

    def arf_in(i, k):
        ref = ar_fin.at[i, quad_u[k]]
        return remote(ref, ref, arf_s.at[i, k - 1], arf_r.at[i, k - 1], quad_dev(k))

    def ar_first(i):
        for k in (3, 2, 1):
            arq(i, k).start()

    def ar_second(i):
        for k in (1, 2, 3):
            arq_in(i, k).wait_recv()
        total = ar_own[i, u]
        for k in (1, 2, 3):
            total += ar_quad[i, quad_u[k]]
        ar_z[i, z] = total
        for k in range(nz - 1, 0, -1):
            arz(i, k).start()

    def ar_third(i):
        for k in range(1, nz):
            arz_in(i, k).wait_recv()
        total = ar_z[i, 0]
        for k in range(1, nz):
            total += ar_z[i, k]
        ar_fin[i, u] = total
        for k in (3, 2, 1):
            arf(i, k).start()

    def ar_last(i, natural, turned):
        for k in (1, 2, 3):
            arf_in(i, k).wait_recv()
        small = jnp.concatenate([ar_fin[i, k] for k in range(4)], axis=1)
        languages = lab_row[...]
        for k in range(LANGS):
            turned[k * RANK : (k + 1) * RANK, :] = jnp.where(languages == own_ref[k], small, 0.0).astype(BF16)
        tall = jnp.concatenate([small] * per, axis=0).T
        labels = lab_col[...]
        for g in range(WIDE // LANES):
            natural[:, g * LANES : (g + 1) * LANES] = jnp.where(
                labels == lane_lang + g * per, tall, 0.0
            ).astype(BF16)

    def mix_blocks(lo, hi):
        def one(i, carry):
            cols = feat((jown + 1 + i) % nb)
            part[:, cols] = nn(hk[...], wk[:, cols]).astype(BF16)
            return carry

        if hi > lo:
            lax.fori_loop(lo, hi, one, 0)

    def mix_own():
        cols = feat(jown)
        part[:, cols] = (nn(hk[...], wk[:, cols]) + lift[...]).astype(BF16)

    load_h.wait()
    load_a.wait()
    h_own = hk[:, unit(c)]
    pick(lambda lo, n: nn(h_own, av[:, lo : lo + n]), 0)
    ar_first(0)

    def rs_z(way, chain, s):
        src = slab(part, zwrap(z - sign(way) * (s + 1)), chain_x(chain), way, chain_cols[chain])
        dst = zr_q.at[way, s] if chain == 2 else zr_p.at[way, s, chain]
        return remote(src, dst, rsz_s.at[way, chain, s], rsz_r.at[way, chain, s], z_dev(sign(way)))

    def rs_q(way, k):
        zs = zwrap(z - sign(way) * (k + 1))
        src = slab(part, zs, 1 - x, way, qcols)
        return remote(src, xr_q.at[zs, way], rsq_s.at[way, k], rsq_r.at[way, k], x_dev)

    def rs_p(way):
        src = slab(part, z, 1 - x, way, pcols)
        return remote(src, xr_p.at[way], rsp_s.at[way], rsp_r.at[way], x_dev)

    def rs_sum(way, chain, s):
        zs = zwrap(z - sign(way) * (s + 1))
        total = slab(part, zs, chain_x(chain), way, chain_cols[chain])[...].astype(F32)
        if chain == 2:
            rs_q(way, s).wait_recv()
            total += xr_q[zs, way].astype(F32)
        if s > 0:
            rs_z(way, chain, s - 1).wait_recv()
            got = zr_q[way, s - 1] if chain == 2 else zr_p[way, s - 1, chain]
            total += got.astype(F32)
        return total

    def rs_ahead(k):
        if k < nz:
            for way in (0, 1):
                rs_q(way, k).start()

    def rs_step(s):
        rs_ahead(s + 2)
        for chain in (1, 2, 0):
            for way in (0, 1):
                if s > 0 or chain == 2:
                    zs = zwrap(z - sign(way) * (s + 1))
                    slab(part, zs, chain_x(chain), way, chain_cols[chain])[...] = rs_sum(way, chain, s).astype(BF16)
                rs_z(way, chain, s).start()

    first_mix = min(1, nz - 2)
    last_mix = max(nz - 3, first_mix)
    spans = last_mix - first_mix + 1
    splits = [(nb - 1) * n // spans for n in range(spans + 1)]

    def shrink_done():
        ar_last(0, sp_nat, sp_t)
        lift[...] = SCALE * nn(sp_nat[...], bv[...])

    for s in range(nz - 2):
        ag_step(s)
        if s == 0:
            ar_second(0)
        if s == first_mix:
            swap_wait(1)[0].wait_recv()
            swap_wait(2)[0].wait_recv()
            pltpu.make_async_copy(wk.at[unit(c), :], wk.at[unit(c), :], load_sem.at[4]).wait()
            load_b.wait()
        if s == min(3, last_mix):
            ar_third(0)
        if s == last_mix:
            shrink_done()
        if s >= first_mix:
            mix_blocks(splits[s - first_mix], splits[s - first_mix + 1])
    mix_own()
    for way in (0, 1):
        for chain in (1, 0):
            rs_z(way, chain, 0).start()
    ag_step(nz - 2)
    for k in (0, 1):
        for way in (0, 1):
            rs_q(way, k).start()

    tile = min(256, units)
    mtile = tokens // 2
    ntiles = units // tile

    def hg_send_copy():
        return remote(hg_send, hg_recv, hg_s, hg_r, core_dev)

    def hg_piece(i):
        part_of, rest = i // (2 * ntiles), i % (2 * ntiles)
        n, m = rest // 2, rest % 2
        owner = c if part_of else 1 - c
        rows_of = pl.ds(aligned(owner * units + n * tile, tile), tile)
        value = nt(gall[m * mtile : (m + 1) * mtile, :], wk[rows_of, :])
        place = (slice(m * mtile, (m + 1) * mtile), slice(n * tile, (n + 1) * tile))
        if part_of:
            hg_own[place] = value
        else:
            hg_send[place] = value.astype(BF16)
        if i == 2 * ntiles - 1:
            hg_send_copy().start()

    pieces = list(range(4 * ntiles))

    def hg_some(count):
        for _ in range(min(count, len(pieces))):
            hg_piece(pieces.pop(0))

    def grads(turned, right, out):
        step = 256

        def one(i, carry):
            at = pl.ds(aligned(i * step, step), step)
            out[at, :] = (SCALE * nn(turned[at, :], right)).astype(BF16)
            return carry

        lax.fori_loop(0, WIDE // step, one, 0)

    sets = ((gb_part, yr_b, xs_b, xr_b, gb_out), (ga_part, yr_a, xs_a, xr_a, ga_out))

    def owner_rows(ref, hh, yy):
        return ref.at[pl.ds(aligned((hh * ny + yy) * own_rows, own_rows), own_rows), :]

    def y_hop(k, hh):
        return k if k in (1, ny - 1) else (ny - 1 if hh else 1)

    relayed = ((1, 0), (3, 1)) if ny == 4 else ()

    def y_copy(i, k, hh):
        src = owner_rows(sets[i][0], hh, (y + k) % ny)
        return remote(src, sets[i][1].at[k - 1, hh], y_s.at[i, k - 1, hh], y_r.at[i, k - 1, hh], y_dev(y_hop(k, hh)))

    def y_send(i):
        for k in (2, 1, 3) if ny == 4 else range(1, ny):
            for hh in (0, 1):
                if (k, hh) not in relayed:
                    y_copy(i, k, hh).start()

    def y_mid(i):
        for k, hh in relayed:
            y_copy(i, 2, hh).wait_recv()
            mine = owner_rows(sets[i][0], hh, (y + k) % ny)
            mine[...] = (mine[...].astype(F32) + sets[i][1][1, hh].astype(F32)).astype(BF16)
            y_copy(i, k, hh).start()

    y_direct = (1, 3) if ny == 4 else tuple(range(1, ny))

    def y_total(i, hh):
        total = owner_rows(sets[i][0], hh, y)[...].astype(F32)
        for k in y_direct:
            total += sets[i][1][k - 1, hh].astype(F32)
        return total

    def h_copy(i):
        return remote(sets[i][2], sets[i][3], xh_s.at[i], xh_r.at[i], h_dev)

    def h_send(i):
        for k in y_direct:
            for hh in (0, 1):
                y_copy(i, k, hh).wait_recv()
        sets[i][2][...] = y_total(i, 1 - h).astype(BF16)
        h_copy(i).start()

    def h_last(i):
        total = y_total(i, h)
        h_copy(i).wait_recv()
        sets[i][4][...] = total + sets[i][3][...].astype(F32)

    for k in range(nz):
        for way in (0, 1):
            ag_q(way, k, 1 - x).wait_recv()
    g_block = gall[:, feat(jown)]
    pick(lambda lo, n: nt(g_block, bv[lo : lo + n, :]), 1)
    ar_first(1)
    for way in (0, 1):
        slab(part, zwrap(z - sign(way)), x, way, qcols)[...] = rs_sum(way, 2, 0).astype(BF16)
        rs_z(way, 2, 0).start()
    rs_ahead(2)
    grads(sp_t, gall[:, feat(jown)], gb_part)
    y_send(0)
    at = {name: min(s, nz - 2) for name, s in dict(second=1, mid_b=2, third=3, back=4, h_b=5, mid_a=6).items()}
    for s in range(1, nz - 1):
        rs_step(s)
        if s == at["second"]:
            ar_second(1)
        if s == at["mid_b"]:
            y_mid(0)
        if s == at["third"]:
            ar_third(1)
        if s == at["back"]:
            ar_last(1, bk_nat, bk_t)
            grads(bk_t, hk[:, unit(c)], ga_part)
            y_send(1)
        else:
            hg_some(2)
        if s == at["h_b"]:
            h_send(0)
        if s == at["mid_a"]:
            y_mid(1)
    hg_some(len(pieces))
    hg_send_copy().wait_recv()
    hg_out[...] = (hg_own[...] + hg_recv[...].astype(F32) + SCALE * nt(bk_nat[...], av[...])).astype(BF16)
    last = nz - 1
    for way in (0, 1):
        slab(part, z, 1 - x, way, pcols)[...] = rs_sum(way, 1, last).astype(BF16)
        rs_p(way).start()
    for way in (0, 1):
        stage[way, :, qcols] = rs_sum(way, 2, last).astype(BF16)
    h_send(1)
    for way in (0, 1):
        total = rs_sum(way, 0, last)
        rs_p(way).wait_recv()
        stage[way, :, pcols] = (total + xr_p[way].astype(F32)).astype(BF16)
    mix_copy = remote(stage.at[1 - c], mixbuf.at[c], mix_s, mix_r, core_dev)
    mix_copy.start()
    h_last(0)
    h_last(1)
    for j in range(nb):
        mixed_out[:, feat(2 * j + c)] = stage[c, :, j * fb : (j + 1) * fb]
    remote(stage.at[c], mixbuf.at[1 - c], mix_s, mix_r, core_dev).wait_recv()
    for j in range(nb):
        mixed_out[:, feat(2 * j + 1 - c)] = mixbuf[1 - c, :, j * fb : (j + 1) * fb]

    for i in range(3):
        swap_wait(i)[1].wait_send()
    for way in (0, 1):
        ag_p(way, x).wait_send()
        rs_p(way).wait_send()
        for k in range(nz):
            ag_q(way, k, x).wait_send()
            rs_q(way, k).wait_send()
        for chain in range(3):
            for s in range(nz - 1):
                ag_z(way, chain, s).wait_send()
                rs_z(way, chain, s).wait_send()
    for i in range(2):
        for k in (1, 2, 3):
            arq(i, k).wait_send()
            arf(i, k).wait_send()
        for k in range(1, nz):
            arz(i, k).wait_send()
        for k in range(1, ny):
            for hh in (0, 1):
                y_copy(i, k, hh).wait_send()
        h_copy(i).wait_send()
    hg_send_copy().wait_send()
    mix_copy.wait_send()


def deliver(*refs):
    n = (len(refs) - 2) // 3
    sources, targets, held = refs[:n], refs[n : 2 * n], refs[2 * n : 3 * n]
    load, store = refs[3 * n :]
    ins = [pltpu.make_async_copy(a, v, load.at[i]) for i, (a, v) in enumerate(zip(sources, held))]
    outs = [pltpu.make_async_copy(v, b, store.at[i]) for i, (v, b) in enumerate(zip(held, targets))]
    for copy in ins:
        copy.start()
    for fetched, stored in zip(ins, outs):
        fetched.wait()
        stored.start()
    for copy in outs:
        copy.wait()


def solution(mesh):
    def body(hidden, down_weight, first, second, grad, labels, owned):
        sz = sizes_of(mesh, hidden, grad)
        nz, ny, nb, fb, fh = sz["nz"], sz["ny"], sz["blocks"], sz["block"], sz["half"]
        rows, tokens, units = sz["rows"], sz["tokens"], sz["units"]
        quarter, own_rows = tokens // 4, WIDE // sz["ndp"]
        pw = sz["early"] * fb
        qw = fh - pw
        dma = pltpu.SemaphoreType.DMA
        vmem = pltpu.VMEM
        hop, kk = nz - 1, max(ny - 1, 1)
        scratch = [
            vmem((2 * units, fh), BF16),
            vmem((tokens, 2 * units), BF16),
            vmem((units, WIDE), BF16),
            vmem((WIDE, fb), BF16),
            vmem((tokens, fh), BF16),
            vmem((tokens, fh), BF16),
            vmem((2, hop, 2, rows, pw), BF16),
            vmem((2, hop, rows, qw), BF16),
            vmem((nz, 2, rows, qw), BF16),
            vmem((2, rows, pw), BF16),
            vmem((2, rows, fh), BF16),
            vmem((2, rows, fh), BF16),
            vmem((tokens, LANES), jnp.int32),
            vmem((2, 4, RANK, quarter), F32),
            vmem((2, 4, RANK, quarter), F32),
            vmem((2, nz, RANK, quarter), F32),
            vmem((2, 4, RANK, quarter), F32),
            vmem((tokens, WIDE), BF16),
            vmem((WIDE, tokens), BF16),
            vmem((tokens, WIDE), BF16),
            vmem((WIDE, tokens), BF16),
            vmem((tokens, fb), F32),
            vmem((tokens, units), F32),
            vmem((tokens, units), BF16),
            vmem((tokens, units), BF16),
            vmem((WIDE, fb), BF16),
            vmem((WIDE, units), BF16),
            vmem((kk, 2, own_rows, fb), BF16),
            vmem((kk, 2, own_rows, units), BF16),
            vmem((own_rows, fb), BF16),
            vmem((own_rows, units), BF16),
            vmem((own_rows, fb), BF16),
            vmem((own_rows, units), BF16),
            dma((5,)), dma((3,)), dma((3,)),
            dma((2, 3, hop)), dma((2, 3, hop)), dma((2,)), dma((2,)), dma((2, nz)), dma((2, nz)),
            dma((2, 3, hop)), dma((2, 3, hop)), dma((2, nz)), dma((2, nz)), dma((2,)), dma((2,)), dma, dma,
            dma((2, 3)), dma((2, 3)), dma((2, hop)), dma((2, hop)), dma((2, 3)), dma((2, 3)),
            dma((2, kk, 2)), dma((2, kk, 2)), dma((2,)), dma((2,)), dma, dma,
        ]
        anywhere = pl.BlockSpec(memory_space=pl.ANY)
        on_chip = pl.BlockSpec(memory_space=pltpu.VMEM)
        mixed, hg, ga, gb = pl.pallas_call(
            functools.partial(kernel, sz),
            out_shape=(
                jax.ShapeDtypeStruct((rows, 2 * fh), BF16),
                jax.ShapeDtypeStruct((tokens, units), BF16),
                jax.ShapeDtypeStruct((own_rows, units), F32),
                jax.ShapeDtypeStruct((own_rows, fb), F32),
            ),
            in_specs=[anywhere] * 5 + [on_chip] + [pl.BlockSpec(memory_space=pltpu.SMEM)],
            out_specs=(on_chip,) * 4,
            scratch_shapes=scratch,
            compiler_params=pltpu.CompilerParams(
                collective_id=0, has_side_effects=True, vmem_limit_bytes=56 * 1024 * 1024
            ),
        )(hidden, down_weight, first, second, grad, labels, owned)
        results = (mixed, hg, ga, gb)
        shapes = [jax.ShapeDtypeStruct(r.shape, r.dtype) for r in results]
        mixed, hg, ga, gb = pl.pallas_call(
            deliver,
            out_shape=shapes,
            in_specs=[anywhere] * 4,
            out_specs=[anywhere] * 4,
            scratch_shapes=[vmem(r.shape, r.dtype) for r in results] + [dma((4,)), dma((4,))],
        )(*results)
        slots = own_rows // RANK
        return mixed, hg, ga.reshape(slots, RANK, units), gb.reshape(slots, RANK, fb)

    in_specs = (
        P("dp", "tensor"),
        P("tensor", None),
        P("tensor", None),
        P(None, "tensor"),
        P(("dp", "tensor"), None),
        P("dp", None),
        P(),
    )
    out_specs = (
        P(("dp", "tensor"), None),
        P("dp", "tensor"),
        P("dp", None, "tensor"),
        P("dp", None, "tensor"),
    )
    return jax.shard_map(body, mesh=mesh, in_specs=in_specs, out_specs=out_specs, check_vma=False)
```
